128 devices in a mesh: dp: 16 (over y_lo, x, core), expert: 8 (over y_hi, z).
Axes of the slice: x: 4, y: 4 (y_hi: 2, y_lo: 2; y = y_hi * 2 + y_lo), z: 4, core: 2. Of those that a mesh axis runs over, the one named last changes fastest.
Arguments:
- out_grad: bfloat16 [16384, 6144], P(('dp', 'expert')), may hold values from -6 to 6
- routes: int32 [16384, 2], P(('dp', 'expert')), may hold values from 0 to 7, all different within a row; in each aligned block of 128 rows (0 to 127, 128 to 255, ...) at most 96 rows name the same one
- probs: bfloat16 [16384, 2], P(('dp', 'expert')), may hold values from 0.099609375 to 0.8984375
- gate_saved: bfloat16 [98304, 1024], P(('dp', 'expert')), may hold values from -6 to 6
- up_saved: bfloat16 [98304, 1024], P(('dp', 'expert')), may hold values from -6 to 6
- weight: float32 [8, 6144, 1024], P('expert', 'dp'), may hold values from -0.078125 to 0.078125
- moment1: float32 [8, 6144, 1024], P('expert', 'dp'), may hold values from -6 to 6
- moment2: float32 [8, 6144, 1024], P('expert', 'dp'), may hold values from 0.5 to 4
Outputs:
- new_weight: float32 [8, 6144, 1024], P('expert', 'dp')
- new_moment1: float32 [8, 6144, 1024], P('expert', 'dp')
- new_moment2: float32 [8, 6144, 1024], P('expert', 'dp')
- gate_grad: bfloat16 [98304, 1024], P(('dp', 'expert'))
- up_grad: bfloat16 [98304, 1024], P(('dp', 'expert'))
- prob_grad: float32 [16384, 2], P(('dp', 'expert'))
The draws below stay inside these ranges and needn't reach their ends.
Inputs may be any that keep to these rules, and one draw needn't show every extreme that they name: `routes`: each row names 2 different experts; every expert is named somewhere. Among the rows of one device no expert is named by more than 96 rows, and in every draw some device names some expert exactly 96 times.
All inputs are finite; a program needn't handle non-finite values.
Results may differ from the reference program's by a relative error of at most 0.008.
Values may be sent and summed in bfloat16 or wider, within the bound.
No kernel may reach another device: no remote copies, remote signals or barrier semaphores. Data moves between devices by JAX's collectives and lax.ppermute only.
A program may use at most 128 MiB of HBM per device.

```python
import math
import jax
import jax.numpy as jnp
import numpy as np
from jax import lax

D = 6144
FF = 1024
TOPK = 2
TOK_DEV = 128
GROUPS = 16
EXPERTS = 8
MOST = 96
TOKENS = 16384
SLOTS = 98304


def shard_levels(rng, dims, pieces, smallest, top_value):
    level = 1.0
    for position, shards_of in pieces:
        steps = jax.random.uniform(jax.random.fold_in(jax.random.fold_in(rng, 6), position), (shards_of,), jnp.float32, smallest / len(pieces), top_value / len(pieces))
        level = level * jnp.repeat(jnp.exp(steps), dims[position] // shards_of).reshape((-1,) + (1,) * (len(dims) - 1 - position))
    return level


def shared_out(own_key, own, number, rows, number_of, top, most, lean):
    order = jax.random.permutation(own_key, number_of)
    crowded, usual = portions_of(number_of, rows * top, most, lean, True), portions_of(number_of, rows * top, most, lean, False)
    places = jnp.arange(number_of)

    def named(tallies, rotation):
        used = int((tallies > 0).sum())
        fixed = max(1, used // 4)
        moved = fixed + (places - fixed + rotation * (used - fixed)) % max(1, number_of - fixed)
        return jnp.zeros((number_of,), jnp.int32).at[order[jnp.where(places < fixed, places, moved)]].set(jnp.asarray(tallies, jnp.int32))

    tallies = jnp.where(number % 4 == 0, named(crowded, number // 4), named(usual, number - number // 4 - 1))
    mixed = jax.random.permutation(jax.random.fold_in(own, 3), number_of)
    source_of, receiver = mixed[0:number_of // 2 * 2:2], mixed[1:number_of // 2 * 2:2]
    slack = jnp.minimum(tallies[source_of] - 1, most - tallies[receiver]) // 2
    slack = jnp.where((source_of == order[0]) | (receiver == order[0]) | (tallies[receiver] == 0), 0, jnp.maximum(slack, 0))
    moved = jax.random.randint(jax.random.fold_in(own, 4), (number_of // 2,), 0, 1 << 20) % (slack + 1)
    tallies = tallies.at[source_of].add(-moved).at[receiver].add(moved)
    labels = jnp.searchsorted(jnp.cumsum(tallies), jnp.arange(rows * top), side="right").astype(jnp.int32)
    listing = labels.reshape(top, rows).T
    listing = listing[jax.random.permutation(jax.random.fold_in(own, 1), rows)]
    rotation = jax.random.randint(jax.random.fold_in(own, 2), (rows, 1), 0, top)
    return jnp.take_along_axis(listing, (jnp.arange(top)[None, :] + rotation) % top, axis=1)


def portions_of(amount, total, bound, skew, full):
    portions = [(1 << 20) // math.isqrt(grade ** skew) + 1 for grade in range(1, amount + 1)]
    largest = bound if full else min(bound, max(-(-total // amount), total * portions[0] // sum(portions)))
    least = 1 if total - largest >= amount - 1 else 0
    counts, rest = [largest] + [least] * (amount - 1), total - largest - least * (amount - 1)
    while rest > 0:
        movable = [i for i in range(1, amount) if counts[i] < largest] or [i for i in range(1, amount) if counts[i] < bound]
        mass, budget = sum([portions[i] for i in movable]), rest
        for i in movable:
            addition = min(bound - counts[i], max(1, budget * portions[i] // mass), rest)
            counts[i] = counts[i] + addition
            rest = rest - addition
    return np.array(counts)


def normal_values(stream_key, dims, spread, bound, cuts=(), kind=jnp.bfloat16):
    entries = spread * jax.random.normal(stream_key, dims, jnp.float32)
    if cuts:
        entries = entries * shard_levels(stream_key, dims, cuts, -0.22, 0.18)
    return jnp.clip(entries, -bound, bound).astype(kind)


def setup_inputs(seed: int = 0) -> dict:
    key_of = jax.random.split(jax.random.key(seed), 9)
    out_grad = normal_values(key_of[0], (TOKENS, D), 1.0, 6.0, ((0, 128),))
    routes_keys = jax.random.split(jax.random.fold_in(key_of[1], 1), TOKENS // TOK_DEV)
    routes_turns = jax.random.permutation(jax.random.fold_in(key_of[1], 3), TOKENS // TOK_DEV)
    routes = jax.vmap(lambda own, number: shared_out(jax.random.fold_in(key_of[1], 2), own, number, TOK_DEV, EXPERTS, TOPK, MOST, 2))(routes_keys, routes_turns).reshape((TOKENS, TOPK))
    probs = jnp.clip(0.099609375 + 0.7988281 * jax.random.uniform(key_of[2], (TOKENS, TOPK), jnp.float32) ** shard_levels(key_of[2], (TOKENS, TOPK), ((0, 128),), -0.2, 0.2), 0.099609375, 0.8984375).astype(jnp.bfloat16)
    gate_saved = normal_values(key_of[3], (SLOTS, FF), 1.0, 6.0, ((0, 128),))
    up_saved = normal_values(key_of[4], (SLOTS, FF), 1.0, 6.0, ((0, 128),))
    weight = normal_values(key_of[5], (EXPERTS, D, FF), D ** -0.5, 0.078125, ((0, 8), (1, 16)), jnp.float32)
    moment1 = normal_values(key_of[6], (EXPERTS, D, FF), 1.0, 6.0, ((0, 8), (1, 16)), jnp.float32)
    moment2 = jnp.clip(jnp.exp(math.log(4.0) - 2.0794415 * jax.random.uniform(key_of[7], (EXPERTS, D, FF), jnp.float32) ** shard_levels(key_of[7], (EXPERTS, D, FF), ((0, 8), (1, 16)), -0.2, 0.2)), 0.5, 4.0)
    return {"out_grad": out_grad, "routes": routes, "probs": probs, "gate_saved": gate_saved, "up_saved": up_saved, "weight": weight, "moment1": moment1, "moment2": moment2}


first_decay = 0.9
second_decay = 0.95
learn_rate = 0.01
weight_decay = 0.1
epsilon = 1e-08
first_correction = 1.0 - 0.9 ** 20
second_correction = 1.0 - 0.95 ** 20

def slot_tables(route_block, prob_block, experts, capacity):
    tokens_here = route_block.shape[0]
    chosen = (route_block[:, :, None] == jnp.arange(experts, dtype=jnp.int32)[None, None, :]).astype(jnp.int32)
    per_token = lax.optimization_barrier(jnp.sum(chosen, axis=1))
    earlier = jnp.cumsum(per_token, axis=0) - per_token
    ranking = lax.optimization_barrier(jnp.sum(chosen * earlier[:, None, :], axis=2)).astype(jnp.int32)
    slot_ids = (route_block * capacity + ranking).astype(jnp.int32)
    flat_slots = slot_ids.reshape(-1)
    token_ids = jnp.repeat(jnp.arange(tokens_here, dtype=jnp.int32), route_block.shape[1])
    token_of_slot = jnp.full((experts * capacity,), tokens_here, jnp.int32).at[flat_slots].set(token_ids)
    prob_of_slot = jnp.zeros((experts * capacity,), prob_block.dtype).at[flat_slots].set(prob_block.reshape(-1))
    return (slot_ids, token_of_slot.reshape(experts, capacity), prob_of_slot.reshape(experts, capacity))

def reference(out_grad, routes, probs, gate_saved, up_saved, weight, moment1, moment2):
    grad_blocks = out_grad.reshape(GROUPS, EXPERTS, TOK_DEV, D)
    route_blocks = routes.reshape(GROUPS, EXPERTS, TOK_DEV, TOPK)
    prob_blocks = probs.reshape(GROUPS, EXPERTS, TOK_DEV, TOPK)
    slot_ids, token_tables, prob_tables = jax.vmap(jax.vmap(lambda route_block, prob_block: slot_tables(route_block, prob_block, EXPERTS, MOST)))(route_blocks, prob_blocks)
    weight_low = weight.astype(jnp.bfloat16)
    gate_blocks = gate_saved.reshape(GROUPS, EXPERTS, EXPERTS * MOST, FF)
    up_blocks = up_saved.reshape(GROUPS, EXPERTS, EXPERTS * MOST, FF)

    def group_step(summed, inputs):
        grads, slot_table, scales, gate_part, up_part = inputs
        slot_rows = jax.vmap(lambda grad_block, slot_index: jnp.take(grad_block, slot_index.reshape(-1), axis=0, mode='fill', fill_value=0))(grads, slot_table)
        slot_rows = slot_rows.reshape(EXPERTS, EXPERTS, MOST, D).transpose(1, 0, 2, 3).reshape(EXPERTS, EXPERTS * MOST, D)
        slot_scale = scales.transpose(1, 0, 2).reshape(EXPERTS, EXPERTS * MOST).astype(jnp.float32)
        gate_value = gate_part.astype(jnp.float32)
        up_value = up_part.astype(jnp.float32)
        sigmoid_gate = jax.nn.sigmoid(gate_value)
        silu_gate = gate_value * sigmoid_gate
        hidden_low = (silu_gate * up_value).astype(jnp.bfloat16)
        back_grad = jnp.einsum('erd,edf->erf', slot_rows.astype(jnp.float32), weight_low.astype(jnp.float32), precision=lax.Precision.HIGHEST)
        slot_prob_grad = lax.optimization_barrier(jnp.sum(hidden_low.astype(jnp.float32) * back_grad, axis=2))
        hidden_grad = slot_scale[:, :, None] * back_grad
        gate_grad = (hidden_grad * up_value * sigmoid_gate * (1.0 + gate_value * (1.0 - sigmoid_gate))).astype(jnp.bfloat16)
        up_grad = (hidden_grad * silu_gate).astype(jnp.bfloat16)
        scaled_rows = (slot_rows.astype(jnp.float32) * slot_scale[:, :, None]).astype(jnp.bfloat16)
        group_part = jnp.einsum('erd,erf->edf', scaled_rows.astype(jnp.float32), hidden_low.astype(jnp.float32), precision=lax.Precision.HIGHEST)
        group_part = lax.optimization_barrier(group_part.astype(jnp.bfloat16)).astype(jnp.float32)
        return (summed + group_part, (gate_grad, up_grad, slot_prob_grad.reshape(EXPERTS, EXPERTS, MOST)))
    initial = jnp.zeros((EXPERTS, D, FF), jnp.float32)
    summed, (gate_all, up_all, prob_slots) = lax.scan(group_step, initial, (grad_blocks, token_tables, prob_tables, gate_blocks, up_blocks))
    prob_flat = prob_slots.transpose(0, 2, 1, 3).reshape(GROUPS, EXPERTS, EXPERTS * MOST)
    prob_grad = jnp.take_along_axis(prob_flat, slot_ids.reshape(GROUPS, EXPERTS, TOK_DEV * TOPK), axis=2).reshape(TOKENS, TOPK)
    gradient = summed / GROUPS
    new_first = first_decay * moment1 + (1.0 - first_decay) * gradient
    new_second = second_decay * moment2 + (1.0 - second_decay) * gradient * gradient
    update = new_first / first_correction / (jnp.sqrt(new_second / second_correction) + epsilon)
    new_weight = weight - learn_rate * (update + weight_decay * weight)
    return (new_weight, new_first, new_second, gate_all.reshape(SLOTS, FF), up_all.reshape(SLOTS, FF), prob_grad)
```

```python
import jax
import jax.numpy as jnp
from jax import lax
from jax.experimental import pallas as pl
from jax.experimental.pallas import tpu as pltpu
from jax.sharding import PartitionSpec as P

first_decay = 0.9
second_decay = 0.95
learn_rate = 0.01
weight_decay = 0.1
epsilon = 1e-08
first_correction = 1.0 - 0.9**20
second_correction = 1.0 - 0.95**20

AXES = ("dp", "expert")
EXPERTS = 8
GROUPS = 16
TOK = 128
CAP = 96
FF = 1024
ROWS = 384
CHUNKS = 3
PART = 128
WIDE = 8 * PART


def device_id(x, y, z, core):
    return ((y % 2) * 8 + x * 2 + core) * EXPERTS + (y // 2) * 4 + z


def pairs(move):
    found = []
    for x in range(4):
        for y in range(4):
            for z in range(4):
                for core in range(2):
                    nx, ny, nz, ncore = move(x, y, z, core)
                    found.append(
                        (device_id(x, y, z, core), device_id(nx % 4, ny % 4, nz % 4, ncore))
                    )
    return found


Z_RING = pairs(lambda x, y, z, c: (x, y, z + 1 - 2 * c, c))
X_RING = pairs(lambda x, y, z, c: (x + 1 - 2 * c, y, z, c))
Y_HALF = pairs(lambda x, y, z, c: (x, y + 2, z, c))
Y_PAIR = pairs(lambda x, y, z, c: (x, y ^ 1, z, c))
CORE = pairs(lambda x, y, z, c: (x, y, z, 1 - c))


def send(value, route):
    return lax.ppermute(value, AXES, route)


def after(value, *others):
    return lax.optimization_barrier((value, *others))[0]


def split_columns(out_grad, blocks):
    def body(blocks_ref, own_in_ref, other_in_ref, *outs):
        for chunk in range(CHUNKS):
            outs[chunk][...] = own_in_ref[:, chunk * PART : (chunk + 1) * PART]
            outs[CHUNKS][chunk] = other_in_ref[:, chunk * PART : (chunk + 1) * PART]

    chunk_spec = pl.BlockSpec((TOK, PART), lambda b, o: (0, b))
    chunk_shape = jax.ShapeDtypeStruct((TOK, WIDE), out_grad.dtype)
    return pl.pallas_call(
        body,
        out_shape=[chunk_shape] * CHUNKS
        + [jax.ShapeDtypeStruct((CHUNKS, TOK, WIDE), out_grad.dtype)],
        grid_spec=pltpu.PrefetchScalarGridSpec(
            num_scalar_prefetch=1,
            grid=(8,),
            in_specs=[
                pl.BlockSpec((TOK, ROWS), lambda b, o: (0, o[b])),
                pl.BlockSpec((TOK, ROWS), lambda b, o: (0, o[8 + b])),
            ],
            out_specs=[chunk_spec] * CHUNKS
            + [pl.BlockSpec((CHUNKS, TOK, PART), lambda b, o: (0, 0, b))],
        ),
        name="split_columns",
    )(blocks, out_grad, out_grad)


def hidden_of(gate, up):
    sigmoid = 1.0 / (1.0 + jnp.exp(-gate))
    silu = gate * sigmoid
    return sigmoid, silu, (silu * up).astype(jnp.bfloat16)


def one_hot(rank_row):
    slots = lax.broadcasted_iota(jnp.int32, (CAP, TOK), 0).astype(jnp.float32)
    return slots == rank_row.astype(jnp.float32)


def token_hidden(order, gate_saved, up_saved, ranks, scales):
    def body(order_ref, gate_ref, up_ref, rank_ref, scale_ref, out_ref):
        _, _, hidden = hidden_of(
            gate_ref[...].astype(jnp.float32), up_ref[...].astype(jnp.float32)
        )
        hot = one_hot(rank_ref[0])
        mixing = jnp.where(hot, scale_ref[0].astype(jnp.float32), 0.0).astype(jnp.bfloat16)
        out_ref[0] = lax.dot_general(
            mixing, hidden, (((0,), (0,)), ((), ())), preferred_element_type=jnp.float32
        ).astype(jnp.bfloat16)

    return pl.pallas_call(
        body,
        out_shape=jax.ShapeDtypeStruct((EXPERTS, TOK, FF), jnp.bfloat16),
        grid_spec=pltpu.PrefetchScalarGridSpec(
            num_scalar_prefetch=1,
            grid=(EXPERTS,),
            in_specs=[
                pl.BlockSpec((CAP, FF), lambda r, o: (o[r], 0)),
                pl.BlockSpec((CAP, FF), lambda r, o: (o[r], 0)),
                pl.BlockSpec((1, 1, TOK), lambda r, o: (o[r], 0, 0)),
                pl.BlockSpec((1, 1, TOK), lambda r, o: (o[r], 0, 0)),
            ],
            out_specs=pl.BlockSpec((1, TOK, FF), lambda r, o: (r, 0, 0)),
        ),
        name="token_hidden",
    )(order, gate_saved, up_saved, ranks, scales)


def slot_grads(order, gate_saved, up_saved, ranks, scales, back_here, back_there):
    def body(
        order_ref, gate_ref, up_ref, rank_ref, scale_ref, here_ref, there_ref, gg_ref, ug_ref, pg_ref
    ):
        gate = gate_ref[...].astype(jnp.float32)
        up = up_ref[...].astype(jnp.float32)
        sigmoid, silu, hidden = hidden_of(gate, up)
        hot = one_hot(rank_ref[0])
        mixing = hot.astype(jnp.bfloat16)
        rows = here_ref[0] + there_ref[0]
        high = rows.astype(jnp.bfloat16)
        low = (rows - high.astype(jnp.float32)).astype(jnp.bfloat16)
        back = jnp.dot(mixing, high, preferred_element_type=jnp.float32) + jnp.dot(
            mixing, low, preferred_element_type=jnp.float32
        )
        scale = jnp.sum(
            jnp.where(hot, scale_ref[0].astype(jnp.float32), 0.0), axis=1, keepdims=True
        )
        prob = jnp.sum(hidden.astype(jnp.float32) * back, axis=1, keepdims=True)
        pg_ref[0] = jnp.sum(jnp.where(hot, prob, 0.0), axis=0, keepdims=True)
        grad = scale * back
        gg_ref[...] = (grad * up * sigmoid * (1.0 + gate * (1.0 - sigmoid))).astype(jnp.bfloat16)
        ug_ref[...] = (grad * silu).astype(jnp.bfloat16)

    slot_spec = pl.BlockSpec((CAP, FF), lambda r, o: (o[r], 0))
    row_spec = pl.BlockSpec((1, 1, TOK), lambda r, o: (o[r], 0, 0))
    tok_spec = pl.BlockSpec((1, TOK, FF), lambda r, o: (r, 0, 0))
    mirror_spec = pl.BlockSpec((1, TOK, FF), lambda r, o: (r // 4 * 4 + (4 - r % 4) % 4, 0, 0))
    slots = jax.ShapeDtypeStruct((EXPERTS * CAP, FF), jnp.bfloat16)
    return pl.pallas_call(
        body,
        out_shape=(slots, slots, jax.ShapeDtypeStruct((EXPERTS, 1, TOK), jnp.float32)),
        grid_spec=pltpu.PrefetchScalarGridSpec(
            num_scalar_prefetch=1,
            grid=(EXPERTS,),
            in_specs=[slot_spec, slot_spec, row_spec, row_spec, tok_spec, mirror_spec],
            out_specs=(slot_spec, slot_spec, row_spec),
        ),
        name="slot_grads",
    )(order, gate_saved, up_saved, ranks, scales, back_here, back_there)


def ring_steps(value, route, tie=()):
    found = []
    for step in range(3):
        value = send(after(value, *tie) if step == 0 and tie else value, route)
        found.append(value)
    return found


def add(*terms):
    return sum(term.astype(jnp.float32) for term in terms)


def reduce_ring(blocks):
    value = blocks[1]
    for step in range(3):
        met = send(value, X_RING)
        if step == 2:
            return add(met, blocks[0])
        value = add(met, blocks[step + 2]).astype(jnp.bfloat16)


def on_device(out_grad, routes, probs, gate_saved, up_saved, weight, moment1, moment2):
    place = lax.axis_index("dp")
    expert = lax.axis_index("expert")
    y_low, x, core = place // 8, (place // 2) % 4, place % 2
    y_high, z = expert // 4, expert % 4

    blocks = jnp.stack(
        [
            ((y_low ^ dy) * 4 + (x - k * (1 - 2 * side)) % 4) * 2 + side
            for side in (core, 1 - core)
            for k in range(4)
            for dy in range(2)
        ]
    ).astype(jnp.int32)
    order = jnp.stack(
        [
            (y_high ^ dy) * 4 + (z - k * (1 - 2 * core)) % 4
            for dy in range(2)
            for k in range(4)
        ]
    ).astype(jnp.int32)

    *own_columns, other_columns = split_columns(out_grad, blocks)
    met = send(other_columns, CORE)
    here = [jnp.concatenate([own_columns[chunk], met[chunk]]) for chunk in range(CHUNKS)]

    weight_low = weight[0].astype(jnp.bfloat16)
    weight_pair = send(weight_low, Y_PAIR)
    near = [weight_low, *ring_steps(weight_low, X_RING)]
    far = [weight_pair, *ring_steps(weight_pair, X_RING)]

    first_half = [here[0]]
    first_half.append(send(here[0], Z_RING))
    pair_one = send(here[1], Y_HALF)
    both_one = [after(jnp.stack([here[1], pair_one]), first_half[1])]
    first_half.append(send(first_half[1], Z_RING))
    first_half.append(send(first_half[2], Z_RING))
    both_one += ring_steps(both_one[0], Z_RING)
    pair_two = send(after(here[2], pair_one), Y_HALF)
    both_two = [after(jnp.stack([here[2], pair_two]), first_half[3])]
    both_two += ring_steps(both_two[0], Z_RING)
    whole_half = jnp.stack(first_half)
    whole_half = jnp.stack([whole_half, send(after(whole_half, pair_two), Y_HALF)])

    tokens = [
        whole_half.reshape(EXPERTS * 2 * TOK, WIDE),
        jnp.stack(both_one, axis=1).reshape(EXPERTS * 2 * TOK, WIDE),
        jnp.stack(both_two, axis=1).reshape(EXPERTS * 2 * TOK, WIDE),
    ]

    member = jnp.sum(
        (routes[:, :, None] == jnp.arange(EXPERTS, dtype=jnp.int32)).astype(jnp.float32), axis=1
    )
    earlier = jnp.tril(jnp.ones((TOK, TOK), jnp.float32), -1)
    rank = jnp.dot(earlier, member)
    rank = jnp.where(member > 0, rank, -1.0)
    share = jnp.sum(
        jnp.where(
            routes[:, :, None] == jnp.arange(EXPERTS, dtype=jnp.int32),
            probs[:, :, None].astype(jnp.float32),
            0.0,
        ),
        axis=1,
    )
    notes = jnp.stack([rank.T, share.T], axis=1).astype(jnp.bfloat16)
    notes = lax.all_to_all(
        after(notes, first_half[1]), "expert", split_axis=0, concat_axis=0, tiled=True
    )
    ranks, scales = notes[:, 0:1], notes[:, 1:2]

    hidden_here = token_hidden(order, gate_saved, up_saved, ranks, scales)
    hidden_there = send(hidden_here, CORE)
    mirror = [dy * 4 + (4 - k) % 4 for dy in range(2) for k in range(4)]
    hidden = jnp.stack(
        [hidden_here, jnp.stack([hidden_there[r] for r in mirror])], axis=1
    ).reshape(EXPERTS * 2 * TOK, FF)

    gathered = jnp.stack([w[k] for k in range(4) for w in (near, far)])
    tokens[1], gathered = lax.optimization_barrier((tokens[1], gathered))

    sums = [None] * CHUNKS
    for chunk in (1, 0, 2):
        product = lax.dot_general(
            tokens[chunk], hidden, (((0,), (0,)), ((), ())), preferred_element_type=jnp.float32
        ).astype(jnp.bfloat16)
        product = product.reshape(4, 2, PART, FF)
        if chunk == 2:
            other = reduce_ring([product[k, 1] for k in range(4)]).astype(jnp.bfloat16)
            mine = reduce_ring([product[k, 0] for k in range(4)])
        else:
            mine, other = reduce_ring([product[k] for k in range(4)])
            other = other.astype(jnp.bfloat16)
        sums[chunk] = mine + send(other, Y_PAIR).astype(jnp.float32)

    back = sum(
        jnp.dot(
            tokens[chunk],
            gathered[:, chunk * PART : (chunk + 1) * PART].reshape(WIDE, FF),
            preferred_element_type=jnp.float32,
        )
        for chunk in (1, 0, 2)
    ).reshape(EXPERTS, 2, TOK, FF)
    back_there = send(back[:, 1], CORE)
    gate_grad, up_grad, prob_rows = slot_grads(
        order, gate_saved, up_saved, ranks, scales, back[:, 0], back_there
    )
    returned = lax.all_to_all(
        prob_rows, "expert", split_axis=0, concat_axis=0, tiled=True
    ).reshape(EXPERTS, TOK)
    prob_grad = jnp.sum(
        jnp.where(
            routes[:, :, None] == jnp.arange(EXPERTS, dtype=jnp.int32), returned.T[:, None, :], 0.0
        ),
        axis=2,
    )

    gradient = jnp.concatenate(sums, axis=0) / GROUPS
    master = weight[0]
    new_first = first_decay * moment1[0] + (1.0 - first_decay) * gradient
    new_second = second_decay * moment2[0] + (1.0 - second_decay) * gradient * gradient
    update = new_first / first_correction / (jnp.sqrt(new_second / second_correction) + epsilon)
    new_weight = master - learn_rate * (update + weight_decay * master)
    return (new_weight[None], new_first[None], new_second[None], gate_grad, up_grad, prob_grad)


def solution(mesh):
    rows = P(("dp", "expert"), None)
    states = P("expert", "dp", None)
    return jax.shard_map(
        on_device,
        mesh=mesh,
        in_specs=(rows, rows, rows, rows, rows, states, states, states),
        out_specs=(states, states, states, rows, rows, rows),
        check_vma=False,
    )
```

```python
import jax
import jax.numpy as jnp
from jax import lax
from jax.experimental import pallas as pl
from jax.experimental.pallas import tpu as pltpu
from jax.sharding import PartitionSpec as P

first_decay = 0.9
second_decay = 0.95
learn_rate = 0.01
weight_decay = 0.1
epsilon = 1e-08
first_correction = 1.0 - 0.9**20
second_correction = 1.0 - 0.95**20

AXES = ("dp", "expert")
EXPERTS = 8
GROUPS = 16
TOK = 128
CAP = 96
FF = 1024
ROWS = 384
CHUNKS = 3
PART = 128
WIDE = 8 * PART


def device_id(x, y, z, core):
    return ((y % 2) * 8 + x * 2 + core) * EXPERTS + (y // 2) * 4 + z


def pairs(move):
    found = []
    for x in range(4):
        for y in range(4):
            for z in range(4):
                for core in range(2):
                    nx, ny, nz, ncore = move(x, y, z, core)
                    found.append(
                        (device_id(x, y, z, core), device_id(nx % 4, ny % 4, nz % 4, ncore))
                    )
    return found


Z_RING = pairs(lambda x, y, z, c: (x, y, z + 1 - 2 * c, c))
X_RING = pairs(lambda x, y, z, c: (x + 1 - 2 * c, y, z, c))
Y_HALF = pairs(lambda x, y, z, c: (x, y + 2, z, c))
Y_PAIR = pairs(lambda x, y, z, c: (x, y ^ 1, z, c))
CORE = pairs(lambda x, y, z, c: (x, y, z, 1 - c))


def send(value, route):
    return lax.ppermute(value, AXES, route)


def after(value, *others):
    return lax.optimization_barrier((value, *others))[0]


def split_columns(out_grad, blocks):
    def body(blocks_ref, own_in_ref, other_in_ref, *outs):
        for chunk in range(CHUNKS):
            outs[chunk][...] = own_in_ref[:, chunk * PART : (chunk + 1) * PART]
            outs[CHUNKS][chunk] = other_in_ref[:, chunk * PART : (chunk + 1) * PART]

    chunk_spec = pl.BlockSpec((TOK, PART), lambda b, o: (0, b))
    chunk_shape = jax.ShapeDtypeStruct((TOK, WIDE), out_grad.dtype)
    return pl.pallas_call(
        body,
        out_shape=[chunk_shape] * CHUNKS
        + [jax.ShapeDtypeStruct((CHUNKS, TOK, WIDE), out_grad.dtype)],
        grid_spec=pltpu.PrefetchScalarGridSpec(
            num_scalar_prefetch=1,
            grid=(8,),
            in_specs=[
                pl.BlockSpec((TOK, ROWS), lambda b, o: (0, o[b])),
                pl.BlockSpec((TOK, ROWS), lambda b, o: (0, o[8 + b])),
            ],
            out_specs=[chunk_spec] * CHUNKS
            + [pl.BlockSpec((CHUNKS, TOK, PART), lambda b, o: (0, 0, b))],
        ),
        name="split_columns",
    )(blocks, out_grad, out_grad)


def hidden_of(gate, up):
    sigmoid = 1.0 / (1.0 + jnp.exp(-gate))
    silu = gate * sigmoid
    return sigmoid, silu, (silu * up).astype(jnp.bfloat16)


def one_hot(rank_row):
    slots = lax.broadcasted_iota(jnp.int32, (CAP, TOK), 0).astype(jnp.float32)
    return slots == rank_row.astype(jnp.float32)


def token_hidden(order, gate_saved, up_saved, ranks, scales):
    def body(order_ref, gate_ref, up_ref, rank_ref, scale_ref, out_ref):
        _, _, hidden = hidden_of(
            gate_ref[...].astype(jnp.float32), up_ref[...].astype(jnp.float32)
        )
        hot = one_hot(rank_ref[0])
        mixing = jnp.where(hot, scale_ref[0].astype(jnp.float32), 0.0).astype(jnp.bfloat16)
        out_ref[0] = lax.dot_general(
            mixing, hidden, (((0,), (0,)), ((), ())), preferred_element_type=jnp.float32
        ).astype(jnp.bfloat16)

    return pl.pallas_call(
        body,
        out_shape=jax.ShapeDtypeStruct((EXPERTS, TOK, FF), jnp.bfloat16),
        grid_spec=pltpu.PrefetchScalarGridSpec(
            num_scalar_prefetch=1,
            grid=(EXPERTS,),
            in_specs=[
                pl.BlockSpec((CAP, FF), lambda r, o: (o[r], 0)),
                pl.BlockSpec((CAP, FF), lambda r, o: (o[r], 0)),
                pl.BlockSpec((1, 1, TOK), lambda r, o: (o[r], 0, 0)),
                pl.BlockSpec((1, 1, TOK), lambda r, o: (o[r], 0, 0)),
            ],
            out_specs=pl.BlockSpec((1, TOK, FF), lambda r, o: (r, 0, 0)),
        ),
        name="token_hidden",
    )(order, gate_saved, up_saved, ranks, scales)


def slot_grads(order, gate_saved, up_saved, ranks, scales, back_here, back_there):
    def body(
        order_ref, gate_ref, up_ref, rank_ref, scale_ref, here_ref, there_ref, gg_ref, ug_ref, pg_ref
    ):
        gate = gate_ref[...].astype(jnp.float32)
        up = up_ref[...].astype(jnp.float32)
        sigmoid, silu, hidden = hidden_of(gate, up)
        hot = one_hot(rank_ref[0])
        mixing = hot.astype(jnp.bfloat16)
        rows = here_ref[0] + there_ref[0]
        high = rows.astype(jnp.bfloat16)
        low = (rows - high.astype(jnp.float32)).astype(jnp.bfloat16)
        back = jnp.dot(mixing, high, preferred_element_type=jnp.float32) + jnp.dot(
            mixing, low, preferred_element_type=jnp.float32
        )
        scale = jnp.sum(
            jnp.where(hot, scale_ref[0].astype(jnp.float32), 0.0), axis=1, keepdims=True
        )
        prob = jnp.sum(hidden.astype(jnp.float32) * back, axis=1, keepdims=True)
        pg_ref[0] = jnp.sum(jnp.where(hot, prob, 0.0), axis=0, keepdims=True)
        grad = scale * back
        gg_ref[...] = (grad * up * sigmoid * (1.0 + gate * (1.0 - sigmoid))).astype(jnp.bfloat16)
        ug_ref[...] = (grad * silu).astype(jnp.bfloat16)

    slot_spec = pl.BlockSpec((CAP, FF), lambda r, o: (o[r], 0))
    row_spec = pl.BlockSpec((1, 1, TOK), lambda r, o: (o[r], 0, 0))
    tok_spec = pl.BlockSpec((1, TOK, FF), lambda r, o: (r, 0, 0))
    mirror_spec = pl.BlockSpec((1, TOK, FF), lambda r, o: (r // 4 * 4 + (4 - r % 4) % 4, 0, 0))
    slots = jax.ShapeDtypeStruct((EXPERTS * CAP, FF), jnp.bfloat16)
    return pl.pallas_call(
        body,
        out_shape=(slots, slots, jax.ShapeDtypeStruct((EXPERTS, 1, TOK), jnp.float32)),
        grid_spec=pltpu.PrefetchScalarGridSpec(
            num_scalar_prefetch=1,
            grid=(EXPERTS,),
            in_specs=[slot_spec, slot_spec, row_spec, row_spec, tok_spec, mirror_spec],
            out_specs=(slot_spec, slot_spec, row_spec),
        ),
        name="slot_grads",
    )(order, gate_saved, up_saved, ranks, scales, back_here, back_there)


def add(*terms):
    return sum(term.astype(jnp.float32) for term in terms)


def reduce_ring(blocks):
    value, first = blocks[1], None
    for step in range(3):
        met = send(value, X_RING)
        first = met if first is None else first
        if step == 2:
            return add(met, blocks[0]), first
        value = add(met, blocks[step + 2]).astype(jnp.bfloat16)


def on_device(out_grad, routes, probs, gate_saved, up_saved, weight, moment1, moment2):
    place = lax.axis_index("dp")
    expert = lax.axis_index("expert")
    y_low, x, core = place // 8, (place // 2) % 4, place % 2
    y_high, z = expert // 4, expert % 4

    blocks = jnp.stack(
        [
            ((y_low ^ dy) * 4 + (x - k * (1 - 2 * side)) % 4) * 2 + side
            for side in (core, 1 - core)
            for k in range(4)
            for dy in range(2)
        ]
    ).astype(jnp.int32)
    order = jnp.stack(
        [
            (y_high ^ dy) * 4 + (z - k * (1 - 2 * core)) % 4
            for dy in range(2)
            for k in range(4)
        ]
    ).astype(jnp.int32)

    member = jnp.sum(
        (routes[:, :, None] == jnp.arange(EXPERTS, dtype=jnp.int32)).astype(jnp.float32), axis=1
    )
    earlier = jnp.tril(jnp.ones((TOK, TOK), jnp.float32), -1)
    rank = jnp.dot(earlier, member)
    rank = jnp.where(member > 0, rank, -1.0)
    share = jnp.sum(
        jnp.where(
            routes[:, :, None] == jnp.arange(EXPERTS, dtype=jnp.int32),
            probs[:, :, None].astype(jnp.float32),
            0.0,
        ),
        axis=1,
    )
    notes = jnp.stack([rank.T, share.T], axis=1).astype(jnp.bfloat16)
    notes = lax.all_to_all(notes, "expert", split_axis=0, concat_axis=0, tiled=True)
    ranks, scales = notes[:, 0:1], notes[:, 1:2]

    hidden_here = token_hidden(order, gate_saved, up_saved, ranks, scales)
    *own_columns, other_columns = split_columns(out_grad, blocks)
    met = send(other_columns, CORE)
    here = [jnp.concatenate([own_columns[chunk], met[chunk]]) for chunk in range(CHUNKS)]

    weight_low = weight[0].astype(jnp.bfloat16)
    weight_pair = send(weight_low, Y_PAIR)
    pair_one = send(here[1], Y_HALF)
    pair_two = send(here[2], Y_HALF)

    near, far = [weight_low], [weight_pair]
    first_half = [here[0]]
    row, column = here[0], weight_low
    for step in range(3):
        row, column, hidden_here = lax.optimization_barrier(
            (send(row, Z_RING), send(column, X_RING), hidden_here)
        )
        first_half.append(row)
        near.append(column)
    whole_half = jnp.stack(first_half)
    whole_half = jnp.stack([whole_half, send(after(whole_half, pair_one, pair_two), Y_HALF)])

    both_one = [after(jnp.stack([here[1], pair_one]), row)]
    row, column = both_one[0], after(weight_pair, column)
    for step in range(3):
        row, column = lax.optimization_barrier((send(row, Z_RING), send(column, X_RING)))
        both_one.append(row)
        far.append(column)
    both_two = [after(jnp.stack([here[2], pair_two]), row)]
    both_two.append(send(both_two[0], Z_RING))

    tokens = [
        whole_half.reshape(EXPERTS * 2 * TOK, WIDE),
        jnp.stack(both_one, axis=1).reshape(EXPERTS * 2 * TOK, WIDE),
    ]

    hidden_there = send(hidden_here, CORE)
    mirror = [dy * 4 + (4 - k) % 4 for dy in range(2) for k in range(4)]
    hidden = jnp.stack(
        [hidden_here, jnp.stack([hidden_there[r] for r in mirror])], axis=1
    ).reshape(EXPERTS * 2 * TOK, FF)

    def weight_term(chunk):
        product = lax.dot_general(
            tokens[chunk], hidden, (((0,), (0,)), ((), ())), preferred_element_type=jnp.float32
        ).astype(jnp.bfloat16)
        return product.reshape(4, 2, PART, FF)

    def back_term(chunk):
        return jnp.dot(
            tokens[chunk],
            gathered[:, chunk * PART : (chunk + 1) * PART].reshape(WIDE, FF),
            preferred_element_type=jnp.float32,
        )

    gathered = jnp.stack([w[k] for k in range(4) for w in (near, far)])
    product_one = weight_term(1)
    row, product_one = lax.optimization_barrier((both_two[1], product_one))
    passed = send(product_one[1], X_RING)
    row, passed = lax.optimization_barrier((send(row, Z_RING), passed))
    both_two.append(row)
    passed = send(add(passed, product_one[2]).astype(jnp.bfloat16), X_RING)
    row, passed = lax.optimization_barrier((send(row, Z_RING), passed))
    both_two.append(row)
    tokens.append(jnp.stack(both_two, axis=1).reshape(EXPERTS * 2 * TOK, WIDE))
    tokens[0] = after(tokens[0], row)
    passed = send(add(passed, product_one[3]).astype(jnp.bfloat16), X_RING)
    mine, other = add(passed, product_one[0])

    sums = [None] * CHUNKS
    sums[1] = mine + send(other.astype(jnp.bfloat16), Y_PAIR).astype(jnp.float32)
    product_zero = weight_term(0)
    (mine, other), met_zero = reduce_ring([product_zero[k] for k in range(4)])
    sums[0] = mine + send(other.astype(jnp.bfloat16), Y_PAIR).astype(jnp.float32)
    product_two = weight_term(2)
    other, met_two = reduce_ring([product_two[k, 1] for k in range(4)])
    mine, met_last = reduce_ring([product_two[k, 0] for k in range(4)])
    sums[2] = mine + send(other.astype(jnp.bfloat16), Y_PAIR).astype(jnp.float32)

    back = back_term(1)
    tokens[0] = after(tokens[0], met_zero, product_two)
    tokens[2] = after(tokens[2], met_two, met_last)
    back = (back + back_term(0) + back_term(2)).reshape(EXPERTS, 2, TOK, FF)
    back_there = send(back[:, 1], CORE)
    gate_grad, up_grad, prob_rows = slot_grads(
        order, gate_saved, up_saved, ranks, scales, back[:, 0], back_there
    )
    returned = lax.all_to_all(
        prob_rows, "expert", split_axis=0, concat_axis=0, tiled=True
    ).reshape(EXPERTS, TOK)
    prob_grad = jnp.sum(
        jnp.where(
            routes[:, :, None] == jnp.arange(EXPERTS, dtype=jnp.int32), returned.T[:, None, :], 0.0
        ),
        axis=2,
    )

    gradient = jnp.concatenate(sums, axis=0) / GROUPS
    master = weight[0]
    new_first = first_decay * moment1[0] + (1.0 - first_decay) * gradient
    new_second = second_decay * moment2[0] + (1.0 - second_decay) * gradient * gradient
    update = new_first / first_correction / (jnp.sqrt(new_second / second_correction) + epsilon)
    new_weight = master - learn_rate * (update + weight_decay * master)
    return (new_weight[None], new_first[None], new_second[None], gate_grad, up_grad, prob_grad)


def solution(mesh):
    rows = P(("dp", "expert"), None)
    states = P("expert", "dp", None)
    return jax.shard_map(
        on_device,
        mesh=mesh,
        in_specs=(rows, rows, rows, rows, rows, states, states, states),
        out_specs=(states, states, states, rows, rows, rows),
        check_vma=False,
    )
```

```python
import jax
import jax.numpy as jnp
from jax import lax
from jax.experimental import pallas as pl
from jax.experimental.pallas import tpu as pltpu
from jax.sharding import PartitionSpec as P

first_decay = 0.9
second_decay = 0.95
learn_rate = 0.01
weight_decay = 0.1
epsilon = 1e-08
first_correction = 1.0 - 0.9**20
second_correction = 1.0 - 0.95**20

AXES = ("dp", "expert")
EXPERTS = 8
GROUPS = 16
TOK = 128
CAP = 96
FF = 1024
ROWS = 384
CHUNKS = 3
PART = 128
WIDE = 8 * PART


def device_id(x, y, z, core):
    return ((y % 2) * 8 + x * 2 + core) * EXPERTS + (y // 2) * 4 + z


def pairs(move):
    found = []
    for x in range(4):
        for y in range(4):
            for z in range(4):
                for core in range(2):
                    nx, ny, nz, ncore = move(x, y, z, core)
                    found.append(
                        (device_id(x, y, z, core), device_id(nx % 4, ny % 4, nz % 4, ncore))
                    )
    return found


Z_RING = pairs(lambda x, y, z, c: (x, y, z + 1 - 2 * c, c))
X_RING = pairs(lambda x, y, z, c: (x + 1 - 2 * c, y, z, c))
Y_HALF = pairs(lambda x, y, z, c: (x, y + 2, z, c))
Y_PAIR = pairs(lambda x, y, z, c: (x, y ^ 1, z, c))
CORE = pairs(lambda x, y, z, c: (x, y, z, 1 - c))


def send(value, route):
    return lax.ppermute(value, AXES, route)


def after(value, *others):
    return lax.optimization_barrier((value, *others))[0]


def split_columns(out_grad, blocks):
    def body(blocks_ref, own_in_ref, other_in_ref, *outs):
        for chunk in range(CHUNKS):
            outs[chunk][...] = own_in_ref[:, chunk * PART : (chunk + 1) * PART]
            outs[CHUNKS][chunk] = other_in_ref[:, chunk * PART : (chunk + 1) * PART]

    chunk_spec = pl.BlockSpec((TOK, PART), lambda b, o: (0, b))
    chunk_shape = jax.ShapeDtypeStruct((TOK, WIDE), out_grad.dtype)
    return pl.pallas_call(
        body,
        out_shape=[chunk_shape] * CHUNKS
        + [jax.ShapeDtypeStruct((CHUNKS, TOK, WIDE), out_grad.dtype)],
        grid_spec=pltpu.PrefetchScalarGridSpec(
            num_scalar_prefetch=1,
            grid=(8,),
            in_specs=[
                pl.BlockSpec((TOK, ROWS), lambda b, o: (0, o[b])),
                pl.BlockSpec((TOK, ROWS), lambda b, o: (0, o[8 + b])),
            ],
            out_specs=[chunk_spec] * CHUNKS
            + [pl.BlockSpec((CHUNKS, TOK, PART), lambda b, o: (0, 0, b))],
        ),
        name="split_columns",
    )(blocks, out_grad, out_grad)


def hidden_of(gate, up):
    sigmoid = 1.0 / (1.0 + jnp.exp(-gate))
    silu = gate * sigmoid
    return sigmoid, silu, (silu * up).astype(jnp.bfloat16)


def one_hot(rank_row):
    slots = lax.broadcasted_iota(jnp.int32, (CAP, TOK), 0).astype(jnp.float32)
    return slots == rank_row.astype(jnp.float32)


def token_hidden(order, gate_saved, up_saved, ranks, scales):
    def body(order_ref, gate_ref, up_ref, rank_ref, scale_ref, out_ref):
        _, _, hidden = hidden_of(
            gate_ref[...].astype(jnp.float32), up_ref[...].astype(jnp.float32)
        )
        hot = one_hot(rank_ref[0])
        mixing = jnp.where(hot, scale_ref[0].astype(jnp.float32), 0.0).astype(jnp.bfloat16)
        out_ref[0] = lax.dot_general(
            mixing, hidden, (((0,), (0,)), ((), ())), preferred_element_type=jnp.float32
        ).astype(jnp.bfloat16)

    return pl.pallas_call(
        body,
        out_shape=jax.ShapeDtypeStruct((EXPERTS, TOK, FF), jnp.bfloat16),
        grid_spec=pltpu.PrefetchScalarGridSpec(
            num_scalar_prefetch=1,
            grid=(EXPERTS,),
            in_specs=[
                pl.BlockSpec((CAP, FF), lambda r, o: (o[r], 0)),
                pl.BlockSpec((CAP, FF), lambda r, o: (o[r], 0)),
                pl.BlockSpec((1, 1, TOK), lambda r, o: (o[r], 0, 0)),
                pl.BlockSpec((1, 1, TOK), lambda r, o: (o[r], 0, 0)),
            ],
            out_specs=pl.BlockSpec((1, TOK, FF), lambda r, o: (r, 0, 0)),
        ),
        name="token_hidden",
    )(order, gate_saved, up_saved, ranks, scales)


def slot_grads(order, gate_saved, up_saved, ranks, scales, back_here, back_there):
    def body(
        order_ref, gate_ref, up_ref, rank_ref, scale_ref, here_ref, there_ref, gg_ref, ug_ref, pg_ref
    ):
        gate = gate_ref[...].astype(jnp.float32)
        up = up_ref[...].astype(jnp.float32)
        sigmoid, silu, hidden = hidden_of(gate, up)
        hot = one_hot(rank_ref[0])
        mixing = hot.astype(jnp.bfloat16)
        rows = here_ref[0] + there_ref[0]
        high = rows.astype(jnp.bfloat16)
        low = (rows - high.astype(jnp.float32)).astype(jnp.bfloat16)
        back = jnp.dot(mixing, high, preferred_element_type=jnp.float32) + jnp.dot(
            mixing, low, preferred_element_type=jnp.float32
        )
        scale = jnp.sum(
            jnp.where(hot, scale_ref[0].astype(jnp.float32), 0.0), axis=1, keepdims=True
        )
        prob = jnp.sum(hidden.astype(jnp.float32) * back, axis=1, keepdims=True)
        pg_ref[0] = jnp.sum(jnp.where(hot, prob, 0.0), axis=0, keepdims=True)
        grad = scale * back
        gg_ref[...] = (grad * up * sigmoid * (1.0 + gate * (1.0 - sigmoid))).astype(jnp.bfloat16)
        ug_ref[...] = (grad * silu).astype(jnp.bfloat16)

    slot_spec = pl.BlockSpec((CAP, FF), lambda r, o: (o[r], 0))
    row_spec = pl.BlockSpec((1, 1, TOK), lambda r, o: (o[r], 0, 0))
    tok_spec = pl.BlockSpec((1, TOK, FF), lambda r, o: (r, 0, 0))
    mirror_spec = pl.BlockSpec((1, TOK, FF), lambda r, o: (r // 4 * 4 + (4 - r % 4) % 4, 0, 0))
    slots = jax.ShapeDtypeStruct((EXPERTS * CAP, FF), jnp.bfloat16)
    return pl.pallas_call(
        body,
        out_shape=(slots, slots, jax.ShapeDtypeStruct((EXPERTS, 1, TOK), jnp.float32)),
        grid_spec=pltpu.PrefetchScalarGridSpec(
            num_scalar_prefetch=1,
            grid=(EXPERTS,),
            in_specs=[slot_spec, slot_spec, row_spec, row_spec, tok_spec, mirror_spec],
            out_specs=(slot_spec, slot_spec, row_spec),
        ),
        name="slot_grads",
    )(order, gate_saved, up_saved, ranks, scales, back_here, back_there)


def ring_steps(value, route, tie=()):
    found = []
    for step in range(3):
        value = send(after(value, *tie) if step == 0 and tie else value, route)
        found.append(value)
    return found


def add(*terms):
    return sum(term.astype(jnp.float32) for term in terms)


def reduce_ring(blocks):
    value, first = blocks[1], None
    for step in range(3):
        met = send(value, X_RING)
        first = met if first is None else first
        if step == 2:
            return add(met, blocks[0]), first
        value = add(met, blocks[step + 2]).astype(jnp.bfloat16)


def on_device(out_grad, routes, probs, gate_saved, up_saved, weight, moment1, moment2):
    place = lax.axis_index("dp")
    expert = lax.axis_index("expert")
    y_low, x, core = place // 8, (place // 2) % 4, place % 2
    y_high, z = expert // 4, expert % 4

    blocks = jnp.stack(
        [
            ((y_low ^ dy) * 4 + (x - k * (1 - 2 * side)) % 4) * 2 + side
            for side in (core, 1 - core)
            for k in range(4)
            for dy in range(2)
        ]
    ).astype(jnp.int32)
    order = jnp.stack(
        [
            (y_high ^ dy) * 4 + (z - k * (1 - 2 * core)) % 4
            for dy in range(2)
            for k in range(4)
        ]
    ).astype(jnp.int32)

    *own_columns, other_columns = split_columns(out_grad, blocks)
    met = send(other_columns, CORE)
    here = [jnp.concatenate([own_columns[chunk], met[chunk]]) for chunk in range(CHUNKS)]

    weight_low = weight[0].astype(jnp.bfloat16)
    weight_pair = send(weight_low, Y_PAIR)
    near = [weight_low, *ring_steps(weight_low, X_RING)]
    far = [weight_pair, *ring_steps(weight_pair, X_RING)]

    first_half = [here[0]]
    first_half.append(send(here[0], Z_RING))
    pair_one = send(here[1], Y_HALF)
    both_one = [after(jnp.stack([here[1], pair_one]), first_half[1])]
    first_half.append(send(first_half[1], Z_RING))
    first_half.append(send(first_half[2], Z_RING))
    both_one += ring_steps(both_one[0], Z_RING)
    pair_two = send(after(here[2], pair_one), Y_HALF)
    both_two = [after(jnp.stack([here[2], pair_two]), first_half[3])]
    both_two += ring_steps(both_two[0], Z_RING)
    whole_half = jnp.stack(first_half)
    whole_half = jnp.stack([whole_half, send(after(whole_half, pair_two), Y_HALF)])

    tokens = [
        whole_half.reshape(EXPERTS * 2 * TOK, WIDE),
        jnp.stack(both_one, axis=1).reshape(EXPERTS * 2 * TOK, WIDE),
        jnp.stack(both_two, axis=1).reshape(EXPERTS * 2 * TOK, WIDE),
    ]

    member = jnp.sum(
        (routes[:, :, None] == jnp.arange(EXPERTS, dtype=jnp.int32)).astype(jnp.float32), axis=1
    )
    earlier = jnp.tril(jnp.ones((TOK, TOK), jnp.float32), -1)
    rank = jnp.dot(earlier, member)
    rank = jnp.where(member > 0, rank, -1.0)
    share = jnp.sum(
        jnp.where(
            routes[:, :, None] == jnp.arange(EXPERTS, dtype=jnp.int32),
            probs[:, :, None].astype(jnp.float32),
            0.0,
        ),
        axis=1,
    )
    notes = jnp.stack([rank.T, share.T], axis=1).astype(jnp.bfloat16)
    notes = lax.all_to_all(
        after(notes, first_half[1]), "expert", split_axis=0, concat_axis=0, tiled=True
    )
    ranks, scales = notes[:, 0:1], notes[:, 1:2]

    hidden_here = token_hidden(order, gate_saved, up_saved, ranks, scales)
    hidden_there = send(hidden_here, CORE)
    mirror = [dy * 4 + (4 - k) % 4 for dy in range(2) for k in range(4)]
    hidden = jnp.stack(
        [hidden_here, jnp.stack([hidden_there[r] for r in mirror])], axis=1
    ).reshape(EXPERTS * 2 * TOK, FF)

    gathered = jnp.stack([w[k] for k in range(4) for w in (near, far)])
    tokens[1], gathered = lax.optimization_barrier((tokens[1], gathered))

    sums = [None] * CHUNKS
    for chunk in (1, 0, 2):
        product = lax.dot_general(
            tokens[chunk], hidden, (((0,), (0,)), ((), ())), preferred_element_type=jnp.float32
        ).astype(jnp.bfloat16)
        product = product.reshape(4, 2, PART, FF)
        if chunk == 2:
            other, met_two = reduce_ring([product[k, 1] for k in range(4)])
            mine, _ = reduce_ring([product[k, 0] for k in range(4)])
            other = other.astype(jnp.bfloat16)
            tokens[1] = after(tokens[1], product)
            tokens[0], tokens[2] = (after(tokens[c], met_two) for c in (0, 2))
        else:
            (mine, other), _ = reduce_ring([product[k] for k in range(4)])
            other = other.astype(jnp.bfloat16)
        sums[chunk] = mine + send(other, Y_PAIR).astype(jnp.float32)

    back = sum(
        jnp.dot(
            tokens[chunk],
            gathered[:, chunk * PART : (chunk + 1) * PART].reshape(WIDE, FF),
            preferred_element_type=jnp.float32,
        )
        for chunk in (1, 0, 2)
    ).reshape(EXPERTS, 2, TOK, FF)
    back_there = send(back[:, 1], CORE)
    gate_grad, up_grad, prob_rows = slot_grads(
        order, gate_saved, up_saved, ranks, scales, back[:, 0], back_there
    )
    returned = lax.all_to_all(
        prob_rows, "expert", split_axis=0, concat_axis=0, tiled=True
    ).reshape(EXPERTS, TOK)
    prob_grad = jnp.sum(
        jnp.where(
            routes[:, :, None] == jnp.arange(EXPERTS, dtype=jnp.int32), returned.T[:, None, :], 0.0
        ),
        axis=2,
    )

    gradient = jnp.concatenate(sums, axis=0) / GROUPS
    master = weight[0]
    new_first = first_decay * moment1[0] + (1.0 - first_decay) * gradient
    new_second = second_decay * moment2[0] + (1.0 - second_decay) * gradient * gradient
    update = new_first / first_correction / (jnp.sqrt(new_second / second_correction) + epsilon)
    new_weight = master - learn_rate * (update + weight_decay * master)
    return (new_weight[None], new_first[None], new_second[None], gate_grad, up_grad, prob_grad)


def solution(mesh):
    rows = P(("dp", "expert"), None)
    states = P("expert", "dp", None)
    return jax.shard_map(
        on_device,
        mesh=mesh,
        in_specs=(rows, rows, rows, rows, rows, states, states, states),
        out_specs=(states, states, states, rows, rows, rows),
        check_vma=False,
    )
```
